256 devices in a mesh: fsdp: 32 (over x_hi, z, core), tp: 8 (over x_lo, y).
Axes of the slice: x: 4 (x_hi: 2, x_lo: 2; x = x_hi * 2 + x_lo), y: 4, z: 8, core: 2. Of those that a mesh axis runs over, the one named last changes fastest.
Arguments:
- hidden: bfloat16 [2048, 26624], P('fsdp', 'tp'), may hold values from -6 to 6
- out_grad: bfloat16 [2048, 16384], P('tp', 'fsdp'), may hold values from -6 to 6
- weight: bfloat16 [26624, 16384], P('tp', 'fsdp'), may hold values from -0.0390625 to 0.0390625
Outputs:
- hidden_grad: bfloat16 [2048, 26624], P('fsdp', 'tp')
- weight_grad: float32 [26624, 16384], P('tp', 'fsdp')
The draws below stay inside these ranges and needn't reach their ends.
All inputs are finite; a program needn't handle non-finite values.
Results may differ from the reference program's by a relative error of at most 0.015.
Values may be sent and summed in bfloat16 or wider, within the bound.
No kernel may reach another device: no remote copies, remote signals or barrier semaphores. Data moves between devices by JAX's collectives and lax.ppermute only.
A program may use at most 128 MiB of HBM per device.

```python
import math
import jax
import jax.numpy as jnp
from jax import lax

D = 16384
FF = 26624
TOKENS = 2048
N_FSDP = 32


def with_spikes(result, rng, source, target, blocks, factor):
    owner, partner = [(jnp.arange(result.shape[axis_at]) // (result.shape[axis_at] // blocks)).reshape([-1 if axis == axis_at else 1 for axis in range(result.ndim)]) for axis_at in (source, target)]
    chosen = jax.random.permutation(rng, blocks)[partner]
    strong = (owner == chosen) | (owner == (partner + blocks // 2) % blocks)
    return jnp.where(strong, factor * result, result)


def steps_of(own_key, extent, pieces, smallest, high):
    def one(position, shards_of):
        draws = jax.random.uniform(jax.random.fold_in(jax.random.fold_in(own_key, 6), position), (shards_of,), jnp.float32, smallest / len(pieces), high / len(pieces))
        return jnp.repeat(jnp.exp(draws), extent[position] // shards_of).reshape((-1,) + (1,) * (len(extent) - position - 1))

    gain = one(*pieces[0])
    for cut in pieces[1:]:
        gain = gain * one(*cut)
    return gain


def gaussian(key, dims, width, limit, pieces=(), held_as=jnp.bfloat16):
    result = jax.random.normal(key, dims, jnp.float32) * width
    if len(pieces) > 0:
        result = steps_of(key, dims, pieces, -0.22, 0.18) * result
    return jnp.clip(result, min=-limit, max=limit).astype(held_as)


def gaussian_with(stream_key, shape, scale, most, split, heavy, held_as=jnp.bfloat16):
    drawn = scale * jax.random.normal(stream_key, shape, jnp.float32)
    if split:
        drawn = drawn * steps_of(stream_key, shape, split, -0.22, 0.18)
    return jnp.clip(with_spikes(drawn, jax.random.fold_in(stream_key, 3), *heavy), -most, most).astype(held_as)


def setup_inputs(seed: int = 0) -> dict:
    streams_of = jax.random.split(jax.random.key(seed), 4)
    hidden = gaussian(streams_of[0], (TOKENS, FF), 1.0, 6.0, ((0, 32), (1, 8)))
    out_grad = gaussian_with(streams_of[1], (TOKENS, D), 1.0, 6.0, ((0, 8), (1, 32)), (1, 0, 32, 2.75))
    weight = gaussian(streams_of[2], (FF, D), FF ** -0.5, 0.0390625, ((0, 8), (1, 32)))
    return dict(hidden=hidden, out_grad=out_grad, weight=weight)


def reference(hidden, out_grad, weight):
    block = D // N_FSDP
    grad_blocks = out_grad.reshape(TOKENS, N_FSDP, block).transpose(1, 0, 2)
    weight_blocks = weight.reshape(FF, N_FSDP, block).transpose(1, 0, 2)

    def add_block(running, pair):
        term = lax.dot_general(pair[0], pair[1], (((1,), (1,)), ((), ())), preferred_element_type=jnp.float32)
        rounded = lax.optimization_barrier(term.astype(jnp.bfloat16))
        return (running + rounded.astype(jnp.float32), None)
    adjoint, unused = lax.scan(add_block, jnp.zeros((TOKENS, FF), jnp.float32), (grad_blocks, weight_blocks))
    hidden_grad = (adjoint + 0.5 * hidden.astype(jnp.float32)).astype(jnp.bfloat16)
    weight_grad = lax.dot_general(hidden, out_grad, (((0,), (0,)), ((), ())), preferred_element_type=jnp.float32)
    weight_grad = weight_grad * (1.0 / math.sqrt(TOKENS))
    return (hidden_grad, weight_grad)
```

```python
import math

import jax
import jax.numpy as jnp
from jax import lax
from jax.sharding import PartitionSpec as P


CHIPS = [(h, z, c) for h in range(2) for z in range(8) for c in range(2)]
LANES = [(a, y) for a in range(2) for y in range(4)]


def fid(h, z, c):
    return (h * 8 + z % 8) * 2 + c


def tid(a, y):
    return a * 4 + y % 4


def z_move(v, k):
    return lax.ppermute(v, "fsdp", [(fid(h, z, c), fid(h, z + k, c)) for h, z, c in CHIPS])


def x_far(v):
    return lax.ppermute(v, "fsdp", [(fid(h, z, c), fid(1 - h, z, c)) for h, z, c in CHIPS])


def core_swap(v):
    return lax.ppermute(v, "fsdp", [(fid(h, z, c), fid(h, z, 1 - c)) for h, z, c in CHIPS])


def y_move(v, k):
    return lax.ppermute(v, "tp", [(tid(a, y), tid(a, y + k)) for a, y in LANES])


def x_near(v):
    return lax.ppermute(v, "tp", [(tid(a, y), tid(1 - a, y)) for a, y in LANES])


def x_cross(v):
    pairs = []
    for h, z, c in CHIPS:
        for a, y in LANES:
            pairs.append((fid(h, z, c) * 8 + tid(a, y), fid(1 - h, z, c) * 8 + tid(1 - a, y)))
    return lax.ppermute(v, ("fsdp", "tp"), pairs)


def pick(v, index, axis):
    return lax.dynamic_index_in_dim(v, index, axis, keepdims=False)


def local(hidden, out_grad, weight):
    me_f = lax.axis_index("fsdp")
    me_t = lax.axis_index("tp")
    h, z, c = me_f >> 4, (me_f >> 1) & 7, me_f & 1
    a, y = me_t >> 2, me_t & 3
    rows, width = hidden.shape
    half = width // 2
    depth = out_grad.shape[1]
    hr = rows // 2
    f32, bf16 = jnp.float32, jnp.bfloat16

    og_near = x_near(out_grad)
    og_cross = x_cross(out_grad)
    og_far = x_far(out_grad)
    hidden_later, og_near, og_cross, og_far = lax.optimization_barrier((hidden, og_near, og_cross, og_far))
    first = jnp.concatenate([out_grad, og_far], axis=1)
    second = jnp.concatenate([og_near, og_cross], axis=1)
    far_hidden = x_far(hidden_later)

    halves = weight.reshape(2, half, depth)
    w_own = pick(halves, h, 0)
    w_sent, _ = lax.optimization_barrier((pick(halves, 1 - h, 0), og_far))
    w_x = x_far(w_sent)
    w_p = core_swap(w_own)
    w_xp = core_swap(w_x)
    w_mine = jnp.concatenate([w_own, w_x], axis=1)
    w_other = jnp.concatenate([w_p, w_xp], axis=1)

    up0, down0 = y_move(first, 1), y_move(first, -1)
    up1, down1 = y_move(second, 1), y_move(second, -1)
    across0, across1 = y_move(up0, 1), y_move(down1, -1)

    def rows_of(pieces, core):
        return jnp.concatenate([pick(p.reshape(2, 2, rows, 2 * depth), core, 1) for p in pieces], axis=0)

    pieces = (first, up0, across0, down0, second, up1, across1, down1)
    mine = rows_of(pieces, c).reshape(16 * rows, 2 * depth)
    sent = [core_swap(rows_of(pieces[i : i + 4], 1 - c)) for i in (0, 4)]
    other = jnp.concatenate(sent, axis=0).reshape(16 * rows, 2 * depth)
    nt = (((1,), (1,)), ((), ()))
    partial = lax.dot_general(mine, w_mine, nt, preferred_element_type=f32)
    partial = (partial + lax.dot_general(other, w_other, nt, preferred_element_type=f32)).astype(bf16)

    def slot(hh, zz):
        zz = zz & 7
        return (((hh ^ a) * 4 + ((y - (zz >> 1)) & 3)) * 2 + (zz & 1)) * rows

    acts = jnp.zeros((16 * rows, width), bf16)
    for hh, src in ((h, hidden), (1 - h, far_hidden)):
        acts = lax.dynamic_update_slice(acts, src, (slot(hh, z), 0))
        up = down = src
        for k in (1, 2, 3):
            up = z_move(up, 1)
            down = z_move(down, -1)
            acts = lax.dynamic_update_slice(acts, up, (slot(hh, z - k), 0))
            acts = lax.dynamic_update_slice(acts, down, (slot(hh, z + k), 0))
        up = z_move(up[:hr], 1)
        down = z_move(down[hr:], -1)
        acts = lax.dynamic_update_slice(acts, up, (slot(hh, z + 4), 0))
        acts = lax.dynamic_update_slice(acts, down, (slot(hh, z + 4) + hr, 0))

    def part(s):
        return jnp.stack([lax.dynamic_slice(partial, (slot(hh, z + s), 0), (rows, half)) for hh in (1 - h, h)])

    opposite = part(4)
    got_up = z_move(opposite[:, :hr], 1).astype(f32)
    got_down = z_move(opposite[:, hr:], -1).astype(f32)
    up, down = part(3).astype(f32), part(-3).astype(f32)
    run_up = jnp.concatenate([up[:, :hr] + got_up, up[:, hr:]], axis=1)
    run_down = jnp.concatenate([down[:, :hr], down[:, hr:] + got_down], axis=1)
    for s in (2, 1, 0):
        got_up = z_move(run_up.astype(bf16), 1).astype(f32)
        got_down = z_move(run_down.astype(bf16), -1).astype(f32)
        if s == 2:
            acts_early, other, got_up = lax.optimization_barrier((acts, other, got_up))
        if s:
            run_up = part(s).astype(f32) + got_up
            run_down = part(-s).astype(f32) + got_down
    total = part(0).astype(f32) + got_up + got_down
    acts, total = lax.optimization_barrier((acts_early, total))
    far_total = x_far(total[0].astype(bf16)).astype(f32)
    adjoint = jnp.concatenate(
        [jnp.where(h == 0, total[1], far_total), jnp.where(h == 0, far_total, total[1])], axis=1
    )
    hidden_grad = (adjoint + 0.5 * hidden.astype(f32)).astype(bf16)

    tn = (((0,), (0,)), ((), ()))
    product = lax.dot_general(acts_early, other[:, :depth], tn, preferred_element_type=f32)
    product = core_swap(product.astype(bf16)).astype(f32)
    product = lax.dot_general(acts, mine[:, :depth], tn, preferred_element_type=f32) + product
    return (hidden_grad, product * (1.0 / math.sqrt(rows * 32)))


def solution(mesh):
    placed = (P("fsdp", "tp"), P("tp", "fsdp"), P("tp", "fsdp"))
    return jax.shard_map(
        local,
        mesh=mesh,
        in_specs=placed,
        out_specs=(P("fsdp", "tp"), P("tp", "fsdp")),
        check_vma=False,
    )
```

```python
import math

import jax
import jax.numpy as jnp
from jax import lax
from jax.sharding import PartitionSpec as P


CHIPS = [(h, z, c) for h in range(2) for z in range(8) for c in range(2)]
LANES = [(a, y) for a in range(2) for y in range(4)]


def fid(h, z, c):
    return (h * 8 + z % 8) * 2 + c


def tid(a, y):
    return a * 4 + y % 4


def z_move(v, k):
    return lax.ppermute(v, "fsdp", [(fid(h, z, c), fid(h, z + k, c)) for h, z, c in CHIPS])


def x_far(v):
    return lax.ppermute(v, "fsdp", [(fid(h, z, c), fid(1 - h, z, c)) for h, z, c in CHIPS])


def core_swap(v):
    return lax.ppermute(v, "fsdp", [(fid(h, z, c), fid(h, z, 1 - c)) for h, z, c in CHIPS])


def y_move(v, k):
    return lax.ppermute(v, "tp", [(tid(a, y), tid(a, y + k)) for a, y in LANES])


def x_near(v):
    return lax.ppermute(v, "tp", [(tid(a, y), tid(1 - a, y)) for a, y in LANES])


def x_cross(v):
    pairs = []
    for h, z, c in CHIPS:
        for a, y in LANES:
            pairs.append((fid(h, z, c) * 8 + tid(a, y), fid(1 - h, z, c) * 8 + tid(1 - a, y)))
    return lax.ppermute(v, ("fsdp", "tp"), pairs)


def pick(v, index, axis):
    return lax.dynamic_index_in_dim(v, index, axis, keepdims=False)


def local(hidden, out_grad, weight):
    me_f = lax.axis_index("fsdp")
    me_t = lax.axis_index("tp")
    h, z, c = me_f >> 4, (me_f >> 1) & 7, me_f & 1
    a, y = me_t >> 2, me_t & 3
    rows, width = hidden.shape
    half = width // 2
    depth = out_grad.shape[1]
    hr = rows // 2
    f32, bf16 = jnp.float32, jnp.bfloat16

    og_near = x_near(out_grad)
    og_cross = x_cross(out_grad)
    og_far = x_far(out_grad)
    first = jnp.concatenate([out_grad, og_far], axis=1)
    second = jnp.concatenate([og_near, og_cross], axis=1)
    far_hidden = x_far(hidden)

    halves = weight.reshape(2, half, depth)
    w_own = pick(halves, h, 0)
    w_x = x_far(pick(halves, 1 - h, 0))
    w_p = core_swap(w_own)
    w_xp = core_swap(w_x)
    w_mine = jnp.concatenate([w_own, w_x], axis=1)
    w_other = jnp.concatenate([w_p, w_xp], axis=1)

    up0, down0 = y_move(first, 1), y_move(first, -1)
    up1, down1 = y_move(second, 1), y_move(second, -1)
    across0, across1 = y_move(up0, 1), y_move(down1, -1)

    def rows_of(pieces, core):
        return jnp.concatenate([pick(p.reshape(2, 2, rows, 2 * depth), core, 1) for p in pieces], axis=0)

    pieces = (first, up0, across0, down0, second, up1, across1, down1)
    mine = rows_of(pieces, c).reshape(16 * rows, 2 * depth)
    sent = [core_swap(rows_of(pieces[i : i + 4], 1 - c)) for i in (0, 4)]
    other = jnp.concatenate(sent, axis=0).reshape(16 * rows, 2 * depth)
    nt = (((1,), (1,)), ((), ()))
    partial = lax.dot_general(mine, w_mine, nt, preferred_element_type=f32)
    partial = (partial + lax.dot_general(other, w_other, nt, preferred_element_type=f32)).astype(bf16)

    def slot(hh, zz):
        zz = zz & 7
        return (((hh ^ a) * 4 + ((y - (zz >> 1)) & 3)) * 2 + (zz & 1)) * rows

    acts = jnp.zeros((16 * rows, width), bf16)
    for hh, src in ((h, hidden), (1 - h, far_hidden)):
        acts = lax.dynamic_update_slice(acts, src, (slot(hh, z), 0))
        up = down = src
        for k in (1, 2, 3):
            up = z_move(up, 1)
            down = z_move(down, -1)
            acts = lax.dynamic_update_slice(acts, up, (slot(hh, z - k), 0))
            acts = lax.dynamic_update_slice(acts, down, (slot(hh, z + k), 0))
        up = z_move(up[:hr], 1)
        down = z_move(down[hr:], -1)
        acts = lax.dynamic_update_slice(acts, up, (slot(hh, z + 4), 0))
        acts = lax.dynamic_update_slice(acts, down, (slot(hh, z + 4) + hr, 0))

    def part(s):
        return jnp.stack([lax.dynamic_slice(partial, (slot(hh, z + s), 0), (rows, half)) for hh in (1 - h, h)])

    opposite = part(4)
    got_up = z_move(opposite[:, :hr], 1).astype(f32)
    got_down = z_move(opposite[:, hr:], -1).astype(f32)
    up, down = part(3).astype(f32), part(-3).astype(f32)
    run_up = jnp.concatenate([up[:, :hr] + got_up, up[:, hr:]], axis=1)
    run_down = jnp.concatenate([down[:, :hr], down[:, hr:] + got_down], axis=1)
    for s in (2, 1, 0):
        got_up = z_move(run_up.astype(bf16), 1).astype(f32)
        got_down = z_move(run_down.astype(bf16), -1).astype(f32)
        if s:
            run_up = part(s).astype(f32) + got_up
            run_down = part(-s).astype(f32) + got_down
    total = part(0).astype(f32) + got_up + got_down
    far_total = x_far(total[0].astype(bf16)).astype(f32)
    adjoint = jnp.concatenate([jnp.where(h == 0, total[1], far_total), jnp.where(h == 0, far_total, total[1])], axis=1)
    hidden_grad = (adjoint + 0.5 * hidden.astype(f32)).astype(bf16)

    tn = (((0,), (0,)), ((), ()))
    product = lax.dot_general(acts, other[:, :depth], tn, preferred_element_type=f32).astype(bf16)
    product = core_swap(product).astype(f32)
    product = lax.dot_general(acts, mine[:, :depth], tn, preferred_element_type=f32) + product
    product = product * (1.0 / math.sqrt(rows * 32))
    return (hidden_grad, product)


def solution(mesh):
    placed = (P("fsdp", "tp"), P("tp", "fsdp"), P("tp", "fsdp"))
    return jax.shard_map(
        local,
        mesh=mesh,
        in_specs=placed,
        out_specs=(P("fsdp", "tp"), P("tp", "fsdp")),
        check_vma=False,
    )
```
